32 devices in a mesh: row: 8 (over z, y), col: 4 (over x, core).
Axes of the slice: x: 2, y: 2, z: 4, core: 2. Of those that a mesh axis runs over, the one named last changes fastest.
Arguments:
- points: float32 [8, 5120], P(None, ('row', 'col')), may hold values from -6 to 6
- sketch: bfloat16 [5120, 256], P(('row', 'col')), may hold values from -0.625 to 0.625
- rank: int32 [5120], P(('row', 'col')), may hold values from 0 to 5119, each once
- boundary: int32 [1], replicated, may hold values from 1280 to 3840
- scales: float32 [8], replicated, may hold values from 1.5 to 4
Outputs:
- basis: float32 [5120, 256], P(('row', 'col'))
- factor: float32 [256, 256], replicated
The draws below stay inside these ranges and needn't reach their ends.
Inputs may be any that keep to these rules, and one draw needn't show every extreme that they name: `rank`: each tree position appears once.
All inputs are finite; a program needn't handle non-finite values.
Results may differ from the reference program's by a relative error of at most 0.0006.
The reference program's roundings to bfloat16 on the way (of `tile`) count: a program that leaves them out, or rounds other values in their place, can miss the bound.
Values may be sent and summed in bfloat16 or wider, within the bound.
A program may use at most 64 MiB of HBM per device.

```python
import math
import jax
import jax.numpy as jnp
from jax import lax

PTS_DEV = 160
DIMS = 8
RANKS = 256
NPTS = 5120
N_COL = 4


def levels(rng, shape, shards, smallest, top_value):
    gain, own = 1.0, jax.random.fold_in(rng, 6)
    for axis_at, blocks in shards:
        draws = jnp.exp(jax.random.uniform(jax.random.fold_in(own, axis_at), (blocks,), jnp.float32, smallest / len(shards), top_value / len(shards)))
        gain = gain * jnp.repeat(draws, shape[axis_at] // blocks).reshape([-1 if axis == axis_at else 1 for axis in range(len(shape))])
    return gain


def centred(stream_key, extent, scale, bound, shards=(), kind=jnp.bfloat16):
    factor_of = levels(stream_key, extent, shards, -0.22, 0.18) if shards else 1.0
    drawn = jax.random.normal(stream_key, extent, jnp.float32) * scale * factor_of
    return jnp.minimum(jnp.maximum(drawn, -bound), bound).astype(kind)


def setup_inputs(seed: int = 0) -> dict:
    seeds = jax.random.split(jax.random.key(seed), 6)
    points = centred(seeds[0], (DIMS, NPTS), 1.0, 6.0, ((1, 32),), jnp.float32)
    sketch = centred(seeds[1], (NPTS, RANKS), (NPTS // 64) ** -0.5, 0.625, ((0, 32),))
    rank = jax.random.permutation(seeds[2], NPTS).astype(jnp.int32)
    boundary = jax.random.randint(seeds[3], (1,), NPTS // 4, 3 * NPTS // 4 + 1).astype(jnp.int32)
    scales = jnp.clip(jnp.exp(jax.random.uniform(seeds[4], (DIMS,), jnp.float32, math.log(1.5), math.log(4.0))), 1.5, 4.0)
    return dict(points=points, sketch=sketch, rank=rank, boundary=boundary, scales=scales)


def reference(points, sketch, rank, boundary, scales):
    scaled = points / scales[:, None]
    sq = jnp.sum(scaled * scaled, axis=0)
    side = (rank >= boundary[0]).astype(jnp.float32)
    block = PTS_DEV * N_COL
    count = NPTS // block

    def one_block(index):
        start = (index * block).astype(jnp.int32)
        tgt = lax.dynamic_slice_in_dim(scaled, start, block, 1)
        tgt_sq = lax.dynamic_slice_in_dim(sq, start, block, 0)
        tgt_side = lax.dynamic_slice_in_dim(side, start, block, 0)
        inner = lax.dot_general(tgt.astype(jnp.float32), scaled.astype(jnp.float32), (((0,), (0,)), ((), ())), precision=lax.Precision.HIGHEST, preferred_element_type=jnp.float32)
        dist = tgt_sq[:, None] + sq[None, :] - 2.0 * inner
        mask = tgt_side[:, None] + side[None, :] - 2.0 * tgt_side[:, None] * side[None, :]
        tile = (jnp.exp(-0.5 * dist) * mask).astype(jnp.bfloat16)
        return jnp.dot(tile.astype(jnp.float32), sketch.astype(jnp.float32), preferred_element_type=jnp.float32)
    sample = lax.map(one_block, jnp.arange(count, dtype=jnp.int32)).reshape(NPTS, RANKS)
    gram = jnp.dot(sample.T.astype(jnp.float32), sample.astype(jnp.float32), precision=lax.Precision.HIGHEST, preferred_element_type=jnp.float32) / jnp.float32(NPTS)
    shift = 0.1 * jnp.trace(gram) / jnp.float32(RANKS)
    factor = jnp.linalg.cholesky(gram + shift * jnp.eye(RANKS, dtype=jnp.float32))
    basis = jax.scipy.linalg.solve_triangular(factor, sample.T, lower=True).T
    return (basis, factor)
```

```python
import functools

import jax
import jax.numpy as jnp
from jax import lax
from jax.experimental import pallas as pl
from jax.experimental.pallas import tpu as pltpu
from jax.sharding import PartitionSpec as P

HIGHEST = lax.Precision.HIGHEST
FAR = 5000.0
VMEM = pl.BlockSpec(memory_space=pltpu.VMEM)
ANY = pl.BlockSpec(memory_space=pl.ANY)


def dot(a, b, dims, precision=HIGHEST):
    return lax.dot_general(
        a, b, (dims, ((), ())), precision=precision, preferred_element_type=jnp.float32
    )


def remote(src, dst, send, recv, row, col):
    return pltpu.make_async_remote_copy(
        src_ref=src,
        dst_ref=dst,
        send_sem=send,
        recv_sem=recv,
        device_id=(row, col),
        device_id_type=pl.DeviceIdType.MESH,
    )


def each(start, stop, step):
    def run(index, carry):
        step(index)
        return carry

    lax.fori_loop(start, stop, run, 0)


def gather_kernel(rows, cols, info, tests, srcs, tgts, bank, s_info, r_info, s_test, r_test, s_tgt, r_tgt, local):
    row, col = lax.axis_index("row"), lax.axis_index("col")
    barrier = pltpu.get_barrier_semaphore()
    each(1, rows, lambda k: pl.semaphore_signal(barrier, 1, device_id=((row + k) % rows, col), device_id_type=pl.DeviceIdType.MESH))
    each(1, cols, lambda k: pl.semaphore_signal(barrier, 1, device_id=(row, (col + k) % cols), device_id_type=pl.DeviceIdType.MESH))
    own = [
        pltpu.make_async_copy(info, srcs.at[row], local.at[0]),
        pltpu.make_async_copy(info, tgts.at[col], local.at[1]),
        pltpu.make_async_copy(tests, bank.at[row], local.at[2]),
    ]
    for copy in own:
        copy.start()
    pl.semaphore_wait(barrier, rows + cols - 2)

    def tgt(k):
        return remote(info, tgts.at[col], s_tgt.at[k], r_tgt.at[k], row, (col + k) % cols)

    def src(k):
        return remote(info, srcs.at[row], s_info.at[k], r_info.at[k], (row + k) % rows, col)

    def test(k):
        return remote(tests, bank.at[row], s_test.at[k], r_test.at[k], (row + k) % rows, col)

    each(1, cols, lambda k: tgt(k).start())
    each(1, rows, lambda k: src(k).start())
    each(1, rows, lambda k: test(k).start())
    each(1, cols, lambda k: tgt(k).wait())
    each(1, rows, lambda k: src(k).wait())
    each(1, rows, lambda k: test(k).wait())
    for copy in own:
        copy.wait()


def gather(info, tests, rows, cols):
    dma = pltpu.SemaphoreType.DMA
    return pl.pallas_call(
        functools.partial(gather_kernel, rows, cols),
        out_shape=(
            jax.ShapeDtypeStruct((rows,) + info.shape, info.dtype),
            jax.ShapeDtypeStruct((cols,) + info.shape, info.dtype),
            jax.ShapeDtypeStruct((rows,) + tests.shape, tests.dtype),
        ),
        in_specs=[ANY, ANY],
        out_specs=(ANY, ANY, ANY),
        scratch_shapes=[dma((rows,)), dma((rows,)), dma((rows,)), dma((rows,)), dma((cols,)), dma((cols,)), dma((3,))],
        compiler_params=pltpu.CompilerParams(collective_id=0, has_side_effects=True),
        name="gather",
    )(info, tests)


def tile_kernel(srcs, tgts, bank, out, left, right):
    cols, depth, local = tgts.shape
    rows = srcs.shape[0]
    for r in range(rows):
        right[:, r * local : (r + 1) * local] = srcs[r]
    sq = 8
    for place in range(cols):
        col = 2 * (place % (cols // 2)) + place // (cols // 2)
        block = tgts[col]
        half, one = block[sq : sq + 1], block[sq + 1 : sq + 2]
        side, other = block[sq + 2 : sq + 3], block[sq + 3 : sq + 4]
        left[:, place * local : (place + 1) * local] = jnp.concatenate(
            [block[:sq], one, half, -FAR * side, -FAR * other, block[sq + 4 :]], axis=0
        )
    step = 128
    source, tests = right[...], bank[...].reshape(rows * local, bank.shape[2])

    def chunk(index):
        start = pl.multiple_of(index * step, step)
        power = dot(left[:, pl.ds(start, step)].T, source, ((1,), (0,)))
        tile = jnp.exp(power).astype(jnp.bfloat16)
        out[pl.ds(start, step), :] = dot(tile, tests, ((1,), (0,)), None)

    each(0, cols * local // step, chunk)


def tiles(srcs, tgts, bank):
    rows, depth, local = srcs.shape
    cols = tgts.shape[0]
    ranks = bank.shape[2]
    return pl.pallas_call(
        tile_kernel,
        out_shape=jax.ShapeDtypeStruct((cols * local, ranks), jnp.float32),
        in_specs=[VMEM, VMEM, VMEM],
        out_specs=VMEM,
        scratch_shapes=[
            pltpu.VMEM((depth, cols * local), jnp.float32),
            pltpu.VMEM((depth, rows * local), jnp.float32),
        ],
        name="tiles",
    )(srcs, tgts, bank)


def reduce_kernel(
    rows, cols, part, sample, gram, pair, stage, far, square, mate, mine, piece, done,
    s_pair, r_pair, s_far, r_far, s_piece, r_piece, s_done, r_done,
):
    row, col = lax.axis_index("row"), lax.axis_index("col")
    half = cols // 2
    count = rows * half
    parity, spot = col % 2, col // 2
    partner = col + 1 - 2 * parity
    index = row * half + spot

    def place(i):
        return i // half, 2 * (i % half) + parity

    barrier = pltpu.get_barrier_semaphore()
    pl.semaphore_signal(barrier, 1, device_id=(row, partner), device_id_type=pl.DeviceIdType.MESH)
    each(1, count, lambda k: pl.semaphore_signal(barrier, 1, device_id=place((index + k) % count), device_id_type=pl.DeviceIdType.MESH))
    pl.semaphore_wait(barrier, count)

    swap = remote(part.at[1 - parity], pair, s_pair.at[0], r_pair.at[0], row, partner)
    swap.start()
    swap.wait()
    stage[...] = part[parity] + pair[...]

    def send(k):
        there = (spot + k) % half
        return remote(stage.at[there], far.at[k], s_far.at[k], r_far.at[k], row, 2 * there + parity)

    each(1, half, lambda k: send(k).start())
    each(1, half, lambda k: send(k).wait())
    total = stage[spot]
    for k in range(1, half):
        total = total + far[k]
    sample[...] = total

    square[...] = dot(total.T, total, ((1,), (0,))).reshape(square.shape)
    swap = remote(square.at[1 - parity], mate, s_pair.at[1], r_pair.at[1], row, partner)
    swap.start()
    swap.wait()
    mine[...] = square[parity] + mate[...]

    def scatter(k):
        there = (index + k) % count
        r, c = place(there)
        return remote(mine.at[there], piece.at[k], s_piece.at[k], r_piece.at[k], r, c)

    each(1, count, lambda k: scatter(k).start())
    each(1, count, lambda k: scatter(k).wait())
    piece[0] = mine[index]
    done[index] = jnp.sum(piece[...], axis=0)

    def collect(k):
        r, c = place((index + k) % count)
        return remote(done.at[index], done.at[index], s_done.at[k], r_done.at[k], r, c)

    each(1, count, lambda k: collect(k).start())
    each(1, count, lambda k: collect(k).wait())
    swap = remote(done, gram.at[parity], s_pair.at[2], r_pair.at[2], row, partner)
    swap.start()
    gram[parity] = done[...]
    swap.wait()


def reduce(part, rows, cols):
    local, ranks = part.shape[0] // cols, part.shape[1]
    half, count = cols // 2, rows * cols // 2
    share = ranks // 2 // count
    f32 = jnp.float32
    dma = pltpu.SemaphoreType.DMA
    sample, gram = pl.pallas_call(
        functools.partial(reduce_kernel, rows, cols),
        out_shape=(
            jax.ShapeDtypeStruct((local, ranks), f32),
            jax.ShapeDtypeStruct((2, count, share, ranks), f32),
        ),
        in_specs=[VMEM],
        out_specs=(VMEM, VMEM),
        scratch_shapes=[
            pltpu.VMEM((half, local, ranks), f32),
            pltpu.VMEM((half, local, ranks), f32),
            pltpu.VMEM((half, local, ranks), f32),
            pltpu.VMEM((2, count, share, ranks), f32),
            pltpu.VMEM((count, share, ranks), f32),
            pltpu.VMEM((count, share, ranks), f32),
            pltpu.VMEM((count, share, ranks), f32),
            pltpu.VMEM((count, share, ranks), f32),
            dma((3,)), dma((3,)), dma((half,)), dma((half,)), dma((count,)), dma((count,)), dma((count,)), dma((count,)),
        ],
        compiler_params=pltpu.CompilerParams(collective_id=1, has_side_effects=True),
        name="reduce",
    )(part.reshape(2, half, local, ranks))
    return sample, gram.reshape(ranks, ranks)


def factor_block(a):
    size, wide = a.shape[0], 8
    lane = lax.broadcasted_iota(jnp.int32, (size, size), 1)
    diag = lane == lax.broadcasted_iota(jnp.int32, (size, size), 0)
    eye = diag.astype(jnp.float32)
    both = [[a[i : i + wide], eye[i : i + wide]] for i in range(0, size, wide)]
    upper, inverse = [], []
    for b in range(size // wide):
        top, side = both[b]
        at = b * wide
        d = [[top[t : t + 1, at + u : at + u + 1] for u in range(wide)] for t in range(wide)]
        low = [[None] * wide for _ in range(wide)]
        inv = []
        for s in range(wide):
            inv.append(1.0 / d[s][s])
            for t in range(s + 1, wide):
                low[t][s] = d[s][t] * inv[s]
                for u in range(t, wide):
                    d[t][u] = d[t][u] - low[t][s] * d[s][u]
        tops, sides = [], []
        for t in range(wide):
            x, y = top[t : t + 1], side[t : t + 1]
            for s in range(t):
                x = x - low[t][s] * tops[s]
                y = y - low[t][s] * sides[s]
            tops.append(x)
            sides.append(y)
        for i in range(b + 1, size // wide):
            x, y = both[i]
            marks = []
            for t in range(wide):
                mark = both[i][0][:, at + t : at + t + 1]
                for s in range(t):
                    mark = mark - low[t][s] * marks[s]
                marks.append(mark)
            for t in range(wide):
                scaled = marks[t] * inv[t]
                x = x - scaled * tops[t]
                y = y - scaled * sides[t]
            both[i] = [x, y]
        roots = [lax.rsqrt(d[t][t]) for t in range(wide)]
        upper += [tops[t] * roots[t] for t in range(wide)]
        inverse += [sides[t] * roots[t] for t in range(wide)]
    keep = lane >= lax.broadcasted_iota(jnp.int32, (size, size), 0)
    return jnp.where(keep, jnp.concatenate(upper, axis=0), 0.0), jnp.concatenate(inverse, axis=0)


def finish_kernel(scale, gram, sample, basis, factor, up, low):
    ranks = gram.shape[0]
    half = ranks // 2
    mean = gram[...] * scale
    same = lax.broadcasted_iota(jnp.int32, (ranks, ranks), 0) == lax.broadcasted_iota(jnp.int32, (ranks, ranks), 1)
    trace = jnp.sum(jnp.sum(jnp.where(same, mean, 0.0), axis=1, keepdims=True), axis=0, keepdims=True)
    factor[...] = jnp.where(same, mean + (0.1 / ranks) * trace, mean)
    cross = factor[:half, half:]

    def one(index):
        start = pl.multiple_of(index * half, half)
        block = factor[pl.ds(start, half), pl.ds(start, half)]
        u, m = factor_block(block)
        up[index] = u
        low[index] = m

        @pl.when(index == 0)
        def _():
            lift = dot(m, cross, ((1,), (0,)))
            up[2] = lift
            factor[half:, half:] = factor[half:, half:] - dot(lift.T, lift, ((1,), (0,)))

    each(0, 2, one)
    lift = up[2]
    first = dot(sample[:, :half], low[0], ((1,), (1,)))
    second = dot(sample[:, half:] - dot(first, lift, ((1,), (0,))), low[1], ((1,), (1,)))
    basis[:, :half] = first
    basis[:, half:] = second
    factor[:half, :half] = up[0].T
    factor[:half, half:] = jnp.zeros((half, half), jnp.float32)
    factor[half:, :half] = lift.T
    factor[half:, half:] = up[1].T


def finish(gram, sample, everyone):
    ranks = gram.shape[0]
    half = ranks // 2
    return pl.pallas_call(
        functools.partial(finish_kernel, 1.0 / everyone),
        out_shape=(
            jax.ShapeDtypeStruct(sample.shape, jnp.float32),
            jax.ShapeDtypeStruct(gram.shape, jnp.float32),
        ),
        in_specs=[VMEM, VMEM],
        out_specs=(VMEM, VMEM),
        scratch_shapes=[pltpu.VMEM((3, half, half), jnp.float32), pltpu.VMEM((2, half, half), jnp.float32)],
        name="finish",
    )(gram, sample)


def body(rows, cols, points, sketch, rank, boundary, scales):
    scaled = points / scales[:, None]
    side = (rank >= boundary[0]).astype(jnp.float32)[None]
    down = -0.5 * jnp.sum(scaled * scaled, axis=0, keepdims=True)
    fill = jnp.zeros((4, points.shape[1]), jnp.float32)
    info = jnp.concatenate([scaled, down, jnp.ones_like(side), side, 1.0 - side, fill], axis=0)
    srcs, tgts, bank = gather(info, sketch, rows, cols)
    sample, gram = reduce(tiles(srcs, tgts, bank), rows, cols)
    return finish(gram, sample, rows * cols * points.shape[1])


def solution(mesh):
    placed = (P(None, ("row", "col")), P(("row", "col"), None), P(("row", "col")), P(), P())
    return jax.shard_map(
        functools.partial(body, mesh.shape["row"], mesh.shape["col"]),
        mesh=mesh,
        in_specs=placed,
        out_specs=(P(("row", "col"), None), P()),
        check_vma=False,
    )
```

```python
import functools

import jax
import jax.numpy as jnp
from jax import lax
from jax.experimental import pallas as pl
from jax.experimental.pallas import tpu as pltpu
from jax.sharding import PartitionSpec as P

HIGHEST = lax.Precision.HIGHEST
FAR = 5000.0
VMEM = pl.BlockSpec(memory_space=pltpu.VMEM)
ANY = pl.BlockSpec(memory_space=pl.ANY)


def dot(a, b, dims, precision=HIGHEST):
    return lax.dot_general(
        a, b, (dims, ((), ())), precision=precision, preferred_element_type=jnp.float32
    )


def remote(src, dst, send, recv, row, col):
    return pltpu.make_async_remote_copy(
        src_ref=src,
        dst_ref=dst,
        send_sem=send,
        recv_sem=recv,
        device_id=(row, col),
        device_id_type=pl.DeviceIdType.MESH,
    )


def each(start, stop, step):
    def run(index, carry):
        step(index)
        return carry

    lax.fori_loop(start, stop, run, 0)


def gather_kernel(rows, cols, info, tests, srcs, tgts, bank, s_info, r_info, s_test, r_test, s_tgt, r_tgt, local):
    row, col = lax.axis_index("row"), lax.axis_index("col")
    barrier = pltpu.get_barrier_semaphore()
    each(1, rows, lambda k: pl.semaphore_signal(barrier, 1, device_id=((row + k) % rows, col), device_id_type=pl.DeviceIdType.MESH))
    each(1, cols, lambda k: pl.semaphore_signal(barrier, 1, device_id=(row, (col + k) % cols), device_id_type=pl.DeviceIdType.MESH))
    own = [
        pltpu.make_async_copy(info, srcs.at[row], local.at[0]),
        pltpu.make_async_copy(info, tgts.at[col], local.at[1]),
        pltpu.make_async_copy(tests, bank.at[row], local.at[2]),
    ]
    for copy in own:
        copy.start()
    pl.semaphore_wait(barrier, rows + cols - 2)

    def tgt(k):
        return remote(info, tgts.at[col], s_tgt.at[k], r_tgt.at[k], row, (col + k) % cols)

    def src(k):
        return remote(info, srcs.at[row], s_info.at[k], r_info.at[k], (row + k) % rows, col)

    def test(k):
        return remote(tests, bank.at[row], s_test.at[k], r_test.at[k], (row + k) % rows, col)

    each(1, cols, lambda k: tgt(k).start())
    each(1, rows, lambda k: src(k).start())
    each(1, rows, lambda k: test(k).start())
    each(1, cols, lambda k: tgt(k).wait())
    each(1, rows, lambda k: src(k).wait())
    each(1, rows, lambda k: test(k).wait())
    for copy in own:
        copy.wait()


def gather(info, tests, rows, cols):
    dma = pltpu.SemaphoreType.DMA
    return pl.pallas_call(
        functools.partial(gather_kernel, rows, cols),
        out_shape=(
            jax.ShapeDtypeStruct((rows,) + info.shape, info.dtype),
            jax.ShapeDtypeStruct((cols,) + info.shape, info.dtype),
            jax.ShapeDtypeStruct((rows,) + tests.shape, tests.dtype),
        ),
        in_specs=[ANY, ANY],
        out_specs=(ANY, ANY, ANY),
        scratch_shapes=[dma((rows,)), dma((rows,)), dma((rows,)), dma((rows,)), dma((cols,)), dma((cols,)), dma((3,))],
        compiler_params=pltpu.CompilerParams(collective_id=0, has_side_effects=True),
        name="gather",
    )(info, tests)


def tile_kernel(srcs, tgts, bank, out, left, right):
    cols, depth, local = tgts.shape
    rows = srcs.shape[0]
    for r in range(rows):
        right[:, r * local : (r + 1) * local] = srcs[r]
    sq = 8
    for place in range(cols):
        col = 2 * (place % (cols // 2)) + place // (cols // 2)
        block = tgts[col]
        half, one = block[sq : sq + 1], block[sq + 1 : sq + 2]
        side, other = block[sq + 2 : sq + 3], block[sq + 3 : sq + 4]
        left[:, place * local : (place + 1) * local] = jnp.concatenate(
            [block[:sq], one, half, -FAR * side, -FAR * other, block[sq + 4 :]], axis=0
        )
    step = 128
    source, tests = right[...], bank[...].reshape(rows * local, bank.shape[2])

    def chunk(index):
        start = pl.multiple_of(index * step, step)
        power = dot(left[:, pl.ds(start, step)].T, source, ((1,), (0,)))
        tile = jnp.exp(power).astype(jnp.bfloat16)
        out[pl.ds(start, step), :] = dot(tile, tests, ((1,), (0,)), None)

    each(0, cols * local // step, chunk)


def tiles(srcs, tgts, bank):
    rows, depth, local = srcs.shape
    cols = tgts.shape[0]
    ranks = bank.shape[2]
    return pl.pallas_call(
        tile_kernel,
        out_shape=jax.ShapeDtypeStruct((cols * local, ranks), jnp.float32),
        in_specs=[VMEM, VMEM, VMEM],
        out_specs=VMEM,
        scratch_shapes=[
            pltpu.VMEM((depth, cols * local), jnp.float32),
            pltpu.VMEM((depth, rows * local), jnp.float32),
        ],
        name="tiles",
    )(srcs, tgts, bank)


def reduce_kernel(
    rows, cols, part, sample, gram, pair, stage, far, square, mate, mine, piece, done,
    s_pair, r_pair, s_far, r_far, s_piece, r_piece, s_done, r_done,
):
    row, col = lax.axis_index("row"), lax.axis_index("col")
    half = cols // 2
    count = rows * half
    parity, spot = col % 2, col // 2
    partner = col + 1 - 2 * parity
    index = row * half + spot

    def place(i):
        return i // half, 2 * (i % half) + parity

    barrier = pltpu.get_barrier_semaphore()
    pl.semaphore_signal(barrier, 1, device_id=(row, partner), device_id_type=pl.DeviceIdType.MESH)
    each(1, count, lambda k: pl.semaphore_signal(barrier, 1, device_id=place((index + k) % count), device_id_type=pl.DeviceIdType.MESH))
    pl.semaphore_wait(barrier, count)

    swap = remote(part.at[1 - parity], pair, s_pair.at[0], r_pair.at[0], row, partner)
    swap.start()
    swap.wait()
    stage[...] = part[parity] + pair[...]

    def send(k):
        there = (spot + k) % half
        return remote(stage.at[there], far.at[k], s_far.at[k], r_far.at[k], row, 2 * there + parity)

    each(1, half, lambda k: send(k).start())
    each(1, half, lambda k: send(k).wait())
    total = stage[spot]
    for k in range(1, half):
        total = total + far[k]
    sample[...] = total

    square[...] = dot(total.T, total, ((1,), (0,))).reshape(square.shape)
    swap = remote(square.at[1 - parity], mate, s_pair.at[1], r_pair.at[1], row, partner)
    swap.start()
    swap.wait()
    mine[...] = square[parity] + mate[...]

    def scatter(k):
        there = (index + k) % count
        r, c = place(there)
        return remote(mine.at[there], piece.at[k], s_piece.at[k], r_piece.at[k], r, c)

    each(1, count, lambda k: scatter(k).start())
    each(1, count, lambda k: scatter(k).wait())
    piece[0] = mine[index]
    done[index] = jnp.sum(piece[...], axis=0)

    def collect(k):
        r, c = place((index + k) % count)
        return remote(done.at[index], done.at[index], s_done.at[k], r_done.at[k], r, c)

    each(1, count, lambda k: collect(k).start())
    each(1, count, lambda k: collect(k).wait())
    swap = remote(done, gram.at[parity], s_pair.at[2], r_pair.at[2], row, partner)
    swap.start()
    gram[parity] = done[...]
    swap.wait()


def reduce(part, rows, cols):
    local, ranks = part.shape[0] // cols, part.shape[1]
    half, count = cols // 2, rows * cols // 2
    share = ranks // 2 // count
    f32 = jnp.float32
    dma = pltpu.SemaphoreType.DMA
    sample, gram = pl.pallas_call(
        functools.partial(reduce_kernel, rows, cols),
        out_shape=(
            jax.ShapeDtypeStruct((local, ranks), f32),
            jax.ShapeDtypeStruct((2, count, share, ranks), f32),
        ),
        in_specs=[VMEM],
        out_specs=(VMEM, VMEM),
        scratch_shapes=[
            pltpu.VMEM((half, local, ranks), f32),
            pltpu.VMEM((half, local, ranks), f32),
            pltpu.VMEM((half, local, ranks), f32),
            pltpu.VMEM((2, count, share, ranks), f32),
            pltpu.VMEM((count, share, ranks), f32),
            pltpu.VMEM((count, share, ranks), f32),
            pltpu.VMEM((count, share, ranks), f32),
            pltpu.VMEM((count, share, ranks), f32),
            dma((3,)), dma((3,)), dma((half,)), dma((half,)), dma((count,)), dma((count,)), dma((count,)), dma((count,)),
        ],
        compiler_params=pltpu.CompilerParams(collective_id=1, has_side_effects=True),
        name="reduce",
    )(part.reshape(2, half, local, ranks))
    return sample, gram.reshape(ranks, ranks)


def factor_block(a):
    size, wide = a.shape[0], 8
    shape = (wide, size)
    lane = lax.broadcasted_iota(jnp.int32, shape, 1)
    line = lax.broadcasted_iota(jnp.int32, shape, 0)

    def spread(x):
        return jnp.broadcast_to(x, shape)

    blocks = [a[i : i + wide] for i in range(0, size, wide)]
    upper, inverse = [], []
    for b in range(size // wide):
        at = b * wide
        inside = (lane >= at) & (lane < at + wide)
        x = blocks[b]
        y = jnp.where(inside, jnp.where(lane - at == line, 1.0, 0.0), x)
        marks = [spread(x[:, at + u : at + u + 1]) for u in range(wide)]
        over, root = jnp.zeros(shape, jnp.float32), jnp.zeros(shape, jnp.float32)
        for s in range(wide):
            pivot = spread(marks[s][s : s + 1])
            inv = 1.0 / pivot
            over = jnp.where(line == s, inv, over)
            root = jnp.where(line == s, pivot, root)
            if s + 1 < wide:
                low = jnp.where(line > s, marks[s] * inv, 0.0)
                for u in range(s + 1, wide):
                    marks[u] = marks[u] - low * spread(marks[u][s : s + 1])
                x = x - low * spread(x[s : s + 1])
                y = y - low * spread(y[s : s + 1])
        z = y * over
        for s in range(wide - 1, 0, -1):
            z = z - jnp.where(line < s, marks[s] * over, 0.0) * spread(z[s : s + 1])
        rows = [spread(z[t : t + 1]) for t in range(wide)]
        for i in range(b + 1, size // wide):
            old = blocks[i]
            parts = [spread(old[:, at + t : at + t + 1]) * rows[t] for t in range(wide)]
            while len(parts) > 1:
                parts = [p + q for p, q in zip(parts[::2], parts[1::2])]
            blocks[i] = jnp.where(inside, 0.0, old) - parts[0]
        root = lax.rsqrt(root)
        upper.append(jnp.where(lane >= at + line, x * root, 0.0))
        inverse.append(jnp.where(lane <= at + line, y * root, 0.0))
    return jnp.concatenate(upper, axis=0), jnp.concatenate(inverse, axis=0)


def finish_kernel(scale, gram, sample, basis, factor, up, low):
    ranks = gram.shape[0]
    half = ranks // 2
    mean = gram[...] * scale
    same = lax.broadcasted_iota(jnp.int32, (ranks, ranks), 0) == lax.broadcasted_iota(jnp.int32, (ranks, ranks), 1)
    trace = jnp.sum(jnp.sum(jnp.where(same, mean, 0.0), axis=1, keepdims=True), axis=0, keepdims=True)
    factor[...] = jnp.where(same, mean + (0.1 / ranks) * trace, mean)
    cross = factor[:half, half:]

    def one(index):
        start = pl.multiple_of(index * half, half)
        block = factor[pl.ds(start, half), pl.ds(start, half)]
        u, m = factor_block(block)
        up[index] = u
        low[index] = m

        @pl.when(index == 0)
        def _():
            lift = dot(m, cross, ((1,), (0,)))
            up[2] = lift
            factor[half:, half:] = factor[half:, half:] - dot(lift.T, lift, ((1,), (0,)))

    each(0, 2, one)
    lift = up[2]
    first = dot(sample[:, :half], low[0], ((1,), (1,)))
    second = dot(sample[:, half:] - dot(first, lift, ((1,), (0,))), low[1], ((1,), (1,)))
    basis[:, :half] = first
    basis[:, half:] = second
    factor[:half, :half] = up[0].T
    factor[:half, half:] = jnp.zeros((half, half), jnp.float32)
    factor[half:, :half] = lift.T
    factor[half:, half:] = up[1].T


def finish(gram, sample, everyone):
    ranks = gram.shape[0]
    half = ranks // 2
    return pl.pallas_call(
        functools.partial(finish_kernel, 1.0 / everyone),
        out_shape=(
            jax.ShapeDtypeStruct(sample.shape, jnp.float32),
            jax.ShapeDtypeStruct(gram.shape, jnp.float32),
        ),
        in_specs=[VMEM, VMEM],
        out_specs=(VMEM, VMEM),
        scratch_shapes=[pltpu.VMEM((3, half, half), jnp.float32), pltpu.VMEM((2, half, half), jnp.float32)],
        name="finish",
    )(gram, sample)


def body(rows, cols, points, sketch, rank, boundary, scales):
    scaled = points / scales[:, None]
    side = (rank >= boundary[0]).astype(jnp.float32)[None]
    down = -0.5 * jnp.sum(scaled * scaled, axis=0, keepdims=True)
    fill = jnp.zeros((4, points.shape[1]), jnp.float32)
    info = jnp.concatenate([scaled, down, jnp.ones_like(side), side, 1.0 - side, fill], axis=0)
    srcs, tgts, bank = gather(info, sketch, rows, cols)
    sample, gram = reduce(tiles(srcs, tgts, bank), rows, cols)
    return finish(gram, sample, rows * cols * points.shape[1])


def solution(mesh):
    placed = (P(None, ("row", "col")), P(("row", "col"), None), P(("row", "col")), P(), P())
    return jax.shard_map(
        functools.partial(body, mesh.shape["row"], mesh.shape["col"]),
        mesh=mesh,
        in_specs=placed,
        out_specs=(P(("row", "col"), None), P()),
        check_vma=False,
    )
```

```python
import functools

import jax
import jax.numpy as jnp
from jax import lax
from jax.experimental import pallas as pl
from jax.experimental.pallas import tpu as pltpu
from jax.sharding import PartitionSpec as P

HIGHEST = lax.Precision.HIGHEST
FAR = 5000.0
VMEM = pl.BlockSpec(memory_space=pltpu.VMEM)


def dot(a, b, dims, precision=HIGHEST):
    return lax.dot_general(
        a, b, (dims, ((), ())), precision=precision, preferred_element_type=jnp.float32
    )


def remote(src, dst, send, recv, row, col):
    return pltpu.make_async_remote_copy(
        src_ref=src,
        dst_ref=dst,
        send_sem=send,
        recv_sem=recv,
        device_id=(row, col),
        device_id_type=pl.DeviceIdType.MESH,
    )


def each(start, stop, step):
    def run(index, carry):
        step(index)
        return carry

    lax.fori_loop(start, stop, run, 0)


def tile_kernel(
    rows, cols, info, tests, out, srcs, tgts, bank, left,
    s_tgt, r_tgt, s_along, r_along, s_info, r_info, s_over, r_over, s_mate, r_mate,
):
    row, col = lax.axis_index("row"), lax.axis_index("col")
    lines = rows // 2
    line, odd = row // 2, row % 2
    mate = row + 1 - 2 * odd
    local = tests.shape[0]

    def at(k):
        return 2 * ((line + k) % lines) + odd

    def origin(k):
        return 2 * ((line + lines - k) % lines) + odd

    barrier = pltpu.get_barrier_semaphore()
    mesh = pl.DeviceIdType.MESH
    each(1, cols, lambda k: pl.semaphore_signal(barrier, 1, device_id=(row, (col + k) % cols), device_id_type=mesh))
    each(1, lines, lambda k: pl.semaphore_signal(barrier, 1, device_id=(at(k), col), device_id_type=mesh))
    pl.semaphore_signal(barrier, 1, device_id=(mate, col), device_id_type=mesh)
    srcs[row] = info[...]
    tgts[col] = info[...]
    bank[row] = tests[...]
    pl.semaphore_wait(barrier, cols + lines - 1)

    def tgt(k):
        return remote(info, tgts.at[col], s_tgt.at[k], r_tgt.at[k], row, (col + k) % cols)

    def along(k):
        return (
            remote(info, srcs.at[row], s_info.at[k], r_info.at[k], at(k), col),
            remote(tests, bank.at[row], s_along.at[k], r_along.at[k], at(k), col),
        )

    def over(k):
        place = origin(k)
        return (
            remote(srcs.at[place], srcs.at[place], s_mate.at[k], r_mate.at[k], mate, col),
            remote(bank.at[place], bank.at[place], s_over.at[k], r_over.at[k], mate, col),
        )

    def first():
        return (
            remote(info, srcs.at[row], s_mate.at[0], r_mate.at[0], mate, col),
            remote(tests, bank.at[row], s_over.at[0], r_over.at[0], mate, col),
        )

    def go(copies):
        for copy in copies:
            copy.start()

    def come(copies):
        for copy in copies:
            copy.wait_recv()

    def leave(copies):
        for copy in copies:
            copy.wait_send()

    each(1, cols, lambda k: tgt(k).start())
    go(first())
    each(1, lines, lambda k: go(along(k)))
    each(1, cols, lambda k: tgt(k).wait())
    sq = 8
    for place in range(cols):
        block = tgts[2 * (place % (cols // 2)) + place // (cols // 2)]
        half, one = block[sq : sq + 1], block[sq + 1 : sq + 2]
        side, other = block[sq + 2 : sq + 3], block[sq + 3 : sq + 4]
        left[place * local : (place + 1) * local, :] = jnp.concatenate(
            [block[:sq], one, half, -FAR * side, -FAR * other, block[sq + 4 :]], axis=0
        ).T
    step = 2 * local

    def add(place, fresh=False):
        source, test = srcs[place], bank[place]

        def chunk(index):
            rows_of = pl.ds(pl.multiple_of(index * step, step), step)
            power = dot(left[rows_of, :], source, ((1,), (0,)))
            tile = jnp.exp(power).astype(jnp.bfloat16)
            term = dot(tile, test, ((1,), (0,)), None)
            out[rows_of, :] = term if fresh else out[rows_of, :] + term

        each(0, cols // 2, chunk)

    add(row, True)

    def turn(k):
        come(along(k))
        go(over(k))
        add(origin(k))
        come(over(k - 1))
        add(origin(k - 1) + 1 - 2 * odd)

    each(1, lines, turn)
    come(over(lines - 1))
    add(origin(lines - 1) + 1 - 2 * odd)
    leave(first())
    each(1, lines, lambda k: leave(along(k) + over(k)))


def tiles(info, tests, rows, cols):
    depth, local = info.shape
    ranks = tests.shape[1]
    lines = rows // 2
    dma = pltpu.SemaphoreType.DMA
    return pl.pallas_call(
        functools.partial(tile_kernel, rows, cols),
        out_shape=jax.ShapeDtypeStruct((cols * local, ranks), jnp.float32),
        in_specs=[VMEM, VMEM],
        out_specs=VMEM,
        scratch_shapes=[
            pltpu.VMEM((rows, depth, local), jnp.float32),
            pltpu.VMEM((cols, depth, local), jnp.float32),
            pltpu.VMEM((rows, local, ranks), tests.dtype),
            pltpu.VMEM((cols * local, depth), jnp.float32),
            dma((cols,)), dma((cols,)),
            dma((lines,)), dma((lines,)), dma((lines,)), dma((lines,)),
            dma((lines,)), dma((lines,)), dma((lines,)), dma((lines,)),
        ],
        compiler_params=pltpu.CompilerParams(collective_id=0, has_side_effects=True),
        name="tiles",
    )(info, tests)


def reduce_kernel(
    rows, cols, part, sample, gram, pair, stage, far, square, mate, mine, piece, done,
    s_pair, r_pair, s_far, r_far, s_mate, r_mate, s_piece, r_piece, s_done, r_done, s_over, r_over,
):
    row, col = lax.axis_index("row"), lax.axis_index("col")
    half = cols // 2
    count = rows * half
    parity, spot = col % 2, col // 2
    partner = col + 1 - 2 * parity
    index = row * half + spot

    def place(i):
        return i // half, 2 * (i % half) + parity

    barrier = pltpu.get_barrier_semaphore()
    pl.semaphore_signal(barrier, 1, device_id=(row, partner), device_id_type=pl.DeviceIdType.MESH)
    each(1, count, lambda k: pl.semaphore_signal(barrier, 1, device_id=place((index + k) % count), device_id_type=pl.DeviceIdType.MESH))
    pl.semaphore_wait(barrier, count)

    def swap(k):
        there = (spot + k) % half
        return remote(part.at[1 - parity, there], pair.at[there], s_pair.at[k], r_pair.at[k], row, partner)

    def send(k):
        there = (spot + k) % half
        return remote(stage.at[there], far.at[k], s_far.at[k], r_far.at[k], row, 2 * there + parity)

    def merge(k):
        there = (spot + k) % half
        swap(k).wait()
        stage[there] = part[parity, there] + pair[there]

    def forward(k):
        merge(k)
        send(k).start()

    each(1, half, lambda k: swap(k).start())
    swap(0).start()
    each(1, half, forward)
    merge(0)
    each(1, half, lambda k: send(k).wait())
    total = stage[spot]
    for k in range(1, half):
        total = total + far[k]
    sample[...] = total

    square[...] = dot(total.T, total, ((1,), (0,))).reshape(square.shape)
    trade = remote(square.at[1 - parity], mate, s_mate.at[0], r_mate.at[0], row, partner)
    trade.start()
    trade.wait()
    mine[...] = square[parity] + mate[...]

    def scatter(k):
        there = (index + k) % count
        r, c = place(there)
        return remote(mine.at[there], piece.at[k], s_piece.at[k], r_piece.at[k], r, c)

    each(1, count, lambda k: scatter(k).start())
    each(1, count, lambda k: scatter(k).wait())
    piece[0] = mine[index]
    done[...] = jnp.sum(piece[...], axis=0)
    gram[parity, index] = done[...]

    def collect(k):
        r, c = place((index + k) % count)
        return remote(done, gram.at[parity, index], s_done.at[k], r_done.at[k], r, c)

    def pass_on(k):
        there = (index + count - k) % count
        return remote(gram.at[parity, there], gram.at[parity, there], s_over.at[k], r_over.at[k], row, partner)

    def relay(k):
        collect(k).wait_recv()
        pass_on(k).start()

    own = remote(done, gram.at[parity, index], s_over.at[0], r_over.at[0], row, partner)
    each(1, count, lambda k: collect(k).start())
    own.start()
    each(1, count, relay)
    own.wait()
    each(1, count, lambda k: pass_on(k).wait())
    each(1, count, lambda k: collect(k).wait_send())


def reduce(part, rows, cols):
    local, ranks = part.shape[0] // cols, part.shape[1]
    half, count = cols // 2, rows * cols // 2
    share = ranks // 2 // count
    f32 = jnp.float32
    dma = pltpu.SemaphoreType.DMA
    sample, gram = pl.pallas_call(
        functools.partial(reduce_kernel, rows, cols),
        out_shape=(
            jax.ShapeDtypeStruct((local, ranks), f32),
            jax.ShapeDtypeStruct((2, count, share, ranks), f32),
        ),
        in_specs=[VMEM],
        out_specs=(VMEM, VMEM),
        scratch_shapes=[
            pltpu.VMEM((half, local, ranks), f32),
            pltpu.VMEM((half, local, ranks), f32),
            pltpu.VMEM((half, local, ranks), f32),
            pltpu.VMEM((2, count, share, ranks), f32),
            pltpu.VMEM((count, share, ranks), f32),
            pltpu.VMEM((count, share, ranks), f32),
            pltpu.VMEM((count, share, ranks), f32),
            pltpu.VMEM((share, ranks), f32),
            dma((half,)), dma((half,)), dma((half,)), dma((half,)), dma((1,)), dma((1,)), dma((count,)), dma((count,)), dma((count,)), dma((count,)), dma((count,)), dma((count,)),
        ],
        compiler_params=pltpu.CompilerParams(collective_id=1, has_side_effects=True),
        name="reduce",
    )(part.reshape(2, half, local, ranks))
    return sample, gram.reshape(ranks, ranks)


def factor_block(a):
    size, wide = a.shape[0], 8
    shape = (wide, size)
    lane = lax.broadcasted_iota(jnp.int32, shape, 1)
    line = lax.broadcasted_iota(jnp.int32, shape, 0)

    def spread(x):
        return jnp.broadcast_to(x, shape)

    blocks = [a[i : i + wide] for i in range(0, size, wide)]
    upper, inverse = [], []
    for b in range(size // wide):
        at = b * wide
        inside = (lane >= at) & (lane < at + wide)
        x = blocks[b]
        y = jnp.where(inside, jnp.where(lane - at == line, 1.0, 0.0), x)
        marks = [spread(x[:, at + u : at + u + 1]) for u in range(wide)]
        over, root = jnp.zeros(shape, jnp.float32), jnp.zeros(shape, jnp.float32)
        for s in range(wide):
            pivot = spread(marks[s][s : s + 1])
            inv = 1.0 / pivot
            over = jnp.where(line == s, inv, over)
            root = jnp.where(line == s, pivot, root)
            if s + 1 < wide:
                low = jnp.where(line > s, marks[s] * inv, 0.0)
                for u in range(s + 1, wide):
                    marks[u] = marks[u] - low * spread(marks[u][s : s + 1])
                x = x - low * spread(x[s : s + 1])
                y = y - low * spread(y[s : s + 1])
        z = y * over
        for s in range(wide - 1, 0, -1):
            z = z - jnp.where(line < s, marks[s] * over, 0.0) * spread(z[s : s + 1])
        rows = [spread(z[t : t + 1]) for t in range(wide)]
        for i in range(b + 1, size // wide):
            old = blocks[i]
            parts = [spread(old[:, at + t : at + t + 1]) * rows[t] for t in range(wide)]
            while len(parts) > 1:
                parts = [p + q for p, q in zip(parts[::2], parts[1::2])]
            blocks[i] = jnp.where(inside, 0.0, old) - parts[0]
        root = lax.rsqrt(root)
        upper.append(jnp.where(lane >= at + line, x * root, 0.0))
        inverse.append(jnp.where(lane <= at + line, y * root, 0.0))
    return jnp.concatenate(upper, axis=0), jnp.concatenate(inverse, axis=0)


def finish_kernel(scale, gram, sample, basis, factor, up, low):
    ranks = gram.shape[0]
    half = ranks // 2
    mean = gram[...] * scale
    same = lax.broadcasted_iota(jnp.int32, (ranks, ranks), 0) == lax.broadcasted_iota(jnp.int32, (ranks, ranks), 1)
    trace = jnp.sum(jnp.sum(jnp.where(same, mean, 0.0), axis=1, keepdims=True), axis=0, keepdims=True)
    factor[...] = jnp.where(same, mean + (0.1 / ranks) * trace, mean)
    cross = factor[:half, half:]

    def one(index):
        start = pl.multiple_of(index * half, half)
        block = factor[pl.ds(start, half), pl.ds(start, half)]
        u, m = factor_block(block)
        up[index] = u
        low[index] = m

        @pl.when(index == 0)
        def _():
            lift = dot(m, cross, ((1,), (0,)))
            up[2] = lift
            factor[half:, half:] = factor[half:, half:] - dot(lift.T, lift, ((1,), (0,)))

    each(0, 2, one)
    lift = up[2]
    first = dot(sample[:, :half], low[0], ((1,), (1,)))
    second = dot(sample[:, half:] - dot(first, lift, ((1,), (0,))), low[1], ((1,), (1,)))
    basis[:, :half] = first
    basis[:, half:] = second
    factor[:half, :half] = up[0].T
    factor[:half, half:] = jnp.zeros((half, half), jnp.float32)
    factor[half:, :half] = lift.T
    factor[half:, half:] = up[1].T


def finish(gram, sample, everyone):
    ranks = gram.shape[0]
    half = ranks // 2
    return pl.pallas_call(
        functools.partial(finish_kernel, 1.0 / everyone),
        out_shape=(
            jax.ShapeDtypeStruct(sample.shape, jnp.float32),
            jax.ShapeDtypeStruct(gram.shape, jnp.float32),
        ),
        in_specs=[VMEM, VMEM],
        out_specs=(VMEM, VMEM),
        scratch_shapes=[pltpu.VMEM((3, half, half), jnp.float32), pltpu.VMEM((2, half, half), jnp.float32)],
        name="finish",
    )(gram, sample)


def body(rows, cols, points, sketch, rank, boundary, scales):
    scaled = points / scales[:, None]
    side = (rank >= boundary[0]).astype(jnp.float32)[None]
    down = -0.5 * jnp.sum(scaled * scaled, axis=0, keepdims=True)
    fill = jnp.zeros((4, points.shape[1]), jnp.float32)
    info = jnp.concatenate([scaled, down, jnp.ones_like(side), side, 1.0 - side, fill], axis=0)
    sample, gram = reduce(tiles(info, sketch, rows, cols), rows, cols)
    return finish(gram, sample, rows * cols * points.shape[1])


def solution(mesh):
    placed = (P(None, ("row", "col")), P(("row", "col"), None), P(("row", "col")), P(), P())
    return jax.shard_map(
        functools.partial(body, mesh.shape["row"], mesh.shape["col"]),
        mesh=mesh,
        in_specs=placed,
        out_specs=(P(("row", "col"), None), P()),
        check_vma=False,
    )
```

```python
import functools

import jax
import jax.numpy as jnp
from jax import lax
from jax.experimental import pallas as pl
from jax.experimental.pallas import tpu as pltpu
from jax.sharding import PartitionSpec as P

HIGHEST = lax.Precision.HIGHEST
FAR = 5000.0
VMEM = pl.BlockSpec(memory_space=pltpu.VMEM)
SMEM = pl.BlockSpec(memory_space=pltpu.SMEM)


def dot(a, b, dims, precision=HIGHEST):
    return lax.dot_general(
        a, b, (dims, ((), ())), precision=precision, preferred_element_type=jnp.float32
    )


def remote(src, dst, send, recv, row, col):
    return pltpu.make_async_remote_copy(
        src_ref=src,
        dst_ref=dst,
        send_sem=send,
        recv_sem=recv,
        device_id=(row, col),
        device_id_type=pl.DeviceIdType.MESH,
    )


def each(start, stop, step):
    def run(index, carry):
        step(index)
        return carry

    lax.fori_loop(start, stop, run, 0)


def tile_kernel(
    rows, cols, points, tests, rank, boundary, scales, out, info, srcs, tgts, bank, left,
    s_tgt, r_tgt, s_along, r_along, s_info, r_info, s_over, r_over, s_mate, r_mate,
):
    row, col = lax.axis_index("row"), lax.axis_index("col")
    lines = rows // 2
    line, odd = row // 2, row % 2
    mate = row + 1 - 2 * odd
    local = tests.shape[0]

    def at(k):
        return 2 * ((line + k) % lines) + odd

    def origin(k):
        return 2 * ((line + lines - k) % lines) + odd

    barrier = pltpu.get_barrier_semaphore()
    mesh = pl.DeviceIdType.MESH
    each(1, cols, lambda k: pl.semaphore_signal(barrier, 1, device_id=(row, (col + k) % cols), device_id_type=mesh))
    each(1, lines, lambda k: pl.semaphore_signal(barrier, 1, device_id=(at(k), col), device_id_type=mesh))
    pl.semaphore_signal(barrier, 1, device_id=(mate, col), device_id_type=mesh)
    sq = points.shape[0]
    spot = lax.broadcasted_iota(jnp.int32, points.shape, 0)
    scale = jnp.ones(points.shape, jnp.float32)
    for i in range(sq):
        scale = jnp.where(spot == i, scales[i], scale)
    scaled = points[...] / scale
    side = jnp.where(rank[...] >= boundary[0], 1.0, 0.0)
    own = jnp.concatenate(
        [
            scaled,
            -0.5 * jnp.sum(scaled * scaled, axis=0, keepdims=True),
            jnp.ones_like(side),
            side,
            1.0 - side,
            jnp.zeros((info.shape[0] - sq - 4, local), jnp.float32),
        ],
        axis=0,
    )
    info[...] = own
    srcs[row] = own
    tgts[col] = own
    bank[row] = tests[...]
    pl.semaphore_wait(barrier, cols + lines - 1)

    def tgt(k):
        return remote(info, tgts.at[col], s_tgt.at[k], r_tgt.at[k], row, (col + k) % cols)

    def along(k):
        return (
            remote(info, srcs.at[row], s_info.at[k], r_info.at[k], at(k), col),
            remote(tests, bank.at[row], s_along.at[k], r_along.at[k], at(k), col),
        )

    def over(k):
        place = origin(k)
        return (
            remote(srcs.at[place], srcs.at[place], s_mate.at[k], r_mate.at[k], mate, col),
            remote(bank.at[place], bank.at[place], s_over.at[k], r_over.at[k], mate, col),
        )

    def first():
        return (
            remote(info, srcs.at[row], s_mate.at[0], r_mate.at[0], mate, col),
            remote(tests, bank.at[row], s_over.at[0], r_over.at[0], mate, col),
        )

    def go(copies):
        for copy in copies:
            copy.start()

    def come(copies):
        for copy in copies:
            copy.wait_recv()

    def leave(copies):
        for copy in copies:
            copy.wait_send()

    each(1, cols, lambda k: tgt(k).start())
    go(first())
    each(1, lines, lambda k: go(along(k)))
    each(1, cols, lambda k: tgt(k).wait())
    for place in range(cols):
        block = tgts[2 * (place % (cols // 2)) + place // (cols // 2)]
        half, one = block[sq : sq + 1], block[sq + 1 : sq + 2]
        side, other = block[sq + 2 : sq + 3], block[sq + 3 : sq + 4]
        left[place * local : (place + 1) * local, :] = jnp.concatenate(
            [block[:sq], one, half, -FAR * side, -FAR * other, block[sq + 4 :]], axis=0
        ).T
    step = 2 * local

    def add(place, fresh=False):
        source, test = srcs[place], bank[place]

        def chunk(index):
            rows_of = pl.ds(pl.multiple_of(index * step, step), step)
            power = dot(left[rows_of, :], source, ((1,), (0,)))
            tile = jnp.exp(power).astype(jnp.bfloat16)
            term = dot(tile, test, ((1,), (0,)), None)
            out[rows_of, :] = term if fresh else out[rows_of, :] + term

        each(0, cols // 2, chunk)

    add(row, True)

    def turn(k):
        come(along(k))
        go(over(k))
        add(origin(k))
        come(over(k - 1))
        add(origin(k - 1) + 1 - 2 * odd)

    each(1, lines, turn)
    come(over(lines - 1))
    add(origin(lines - 1) + 1 - 2 * odd)
    leave(first())
    each(1, lines, lambda k: leave(along(k) + over(k)))


def tiles(points, tests, rank, boundary, scales, rows, cols):
    depth, local = 8 * ((points.shape[0] + 11) // 8), points.shape[1]
    ranks = tests.shape[1]
    lines = rows // 2
    dma = pltpu.SemaphoreType.DMA
    return pl.pallas_call(
        functools.partial(tile_kernel, rows, cols),
        out_shape=jax.ShapeDtypeStruct((cols * local, ranks), jnp.float32),
        in_specs=[VMEM, VMEM, VMEM, SMEM, SMEM],
        out_specs=VMEM,
        scratch_shapes=[
            pltpu.VMEM((depth, local), jnp.float32),
            pltpu.VMEM((rows, depth, local), jnp.float32),
            pltpu.VMEM((cols, depth, local), jnp.float32),
            pltpu.VMEM((rows, local, ranks), tests.dtype),
            pltpu.VMEM((cols * local, depth), jnp.float32),
            dma((cols,)), dma((cols,)),
            dma((lines,)), dma((lines,)), dma((lines,)), dma((lines,)),
            dma((lines,)), dma((lines,)), dma((lines,)), dma((lines,)),
        ],
        compiler_params=pltpu.CompilerParams(collective_id=0, has_side_effects=True),
        name="tiles",
    )(points, tests, rank[None], boundary, scales)


def reduce_kernel(
    rows, cols, part, sample, gram, pair, stage, far, square, mate, mine, piece, done,
    s_pair, r_pair, s_far, r_far, s_mate, r_mate, s_piece, r_piece, s_done, r_done, s_over, r_over,
):
    row, col = lax.axis_index("row"), lax.axis_index("col")
    half = cols // 2
    count = rows * half
    parity, spot = col % 2, col // 2
    partner = col + 1 - 2 * parity
    index = row * half + spot

    def place(i):
        return i // half, 2 * (i % half) + parity

    barrier = pltpu.get_barrier_semaphore()
    pl.semaphore_signal(barrier, 1, device_id=(row, partner), device_id_type=pl.DeviceIdType.MESH)
    each(1, count, lambda k: pl.semaphore_signal(barrier, 1, device_id=place((index + k) % count), device_id_type=pl.DeviceIdType.MESH))
    pl.semaphore_wait(barrier, count)

    def swap(k):
        there = (spot + k) % half
        return remote(part.at[1 - parity, there], pair.at[there], s_pair.at[k], r_pair.at[k], row, partner)

    def send(k):
        there = (spot + k) % half
        return remote(stage.at[there], far.at[k], s_far.at[k], r_far.at[k], row, 2 * there + parity)

    def merge(k):
        there = (spot + k) % half
        swap(k).wait()
        stage[there] = part[parity, there] + pair[there]

    def forward(k):
        merge(k)
        send(k).start()

    each(1, half, lambda k: swap(k).start())
    swap(0).start()
    each(1, half, forward)
    merge(0)
    each(1, half, lambda k: send(k).wait())
    total = stage[spot]
    for k in range(1, half):
        total = total + far[k]
    sample[...] = total

    square[...] = dot(total.T, total, ((1,), (0,))).reshape(square.shape)
    trade = remote(square.at[1 - parity], mate, s_mate.at[0], r_mate.at[0], row, partner)
    trade.start()
    trade.wait()
    mine[...] = square[parity] + mate[...]

    def scatter(k):
        there = (index + k) % count
        r, c = place(there)
        return remote(mine.at[there], piece.at[k], s_piece.at[k], r_piece.at[k], r, c)

    each(1, count, lambda k: scatter(k).start())
    each(1, count, lambda k: scatter(k).wait())
    piece[0] = mine[index]
    done[...] = jnp.sum(piece[...], axis=0)
    gram[parity, index] = done[...]

    def collect(k):
        r, c = place((index + k) % count)
        return remote(done, gram.at[parity, index], s_done.at[k], r_done.at[k], r, c)

    def pass_on(k):
        there = (index + count - k) % count
        return remote(gram.at[parity, there], gram.at[parity, there], s_over.at[k], r_over.at[k], row, partner)

    def relay(k):
        collect(k).wait_recv()
        pass_on(k).start()

    own = remote(done, gram.at[parity, index], s_over.at[0], r_over.at[0], row, partner)
    each(1, count, lambda k: collect(k).start())
    own.start()
    each(1, count, relay)
    own.wait()
    each(1, count, lambda k: pass_on(k).wait())
    each(1, count, lambda k: collect(k).wait_send())


def reduce(part, rows, cols):
    local, ranks = part.shape[0] // cols, part.shape[1]
    half, count = cols // 2, rows * cols // 2
    share = ranks // 2 // count
    f32 = jnp.float32
    dma = pltpu.SemaphoreType.DMA
    sample, gram = pl.pallas_call(
        functools.partial(reduce_kernel, rows, cols),
        out_shape=(
            jax.ShapeDtypeStruct((local, ranks), f32),
            jax.ShapeDtypeStruct((2, count, share, ranks), f32),
        ),
        in_specs=[VMEM],
        out_specs=(VMEM, VMEM),
        scratch_shapes=[
            pltpu.VMEM((half, local, ranks), f32),
            pltpu.VMEM((half, local, ranks), f32),
            pltpu.VMEM((half, local, ranks), f32),
            pltpu.VMEM((2, count, share, ranks), f32),
            pltpu.VMEM((count, share, ranks), f32),
            pltpu.VMEM((count, share, ranks), f32),
            pltpu.VMEM((count, share, ranks), f32),
            pltpu.VMEM((share, ranks), f32),
            dma((half,)), dma((half,)), dma((half,)), dma((half,)), dma((1,)), dma((1,)), dma((count,)), dma((count,)), dma((count,)), dma((count,)), dma((count,)), dma((count,)),
        ],
        compiler_params=pltpu.CompilerParams(collective_id=1, has_side_effects=True),
        name="reduce",
    )(part.reshape(2, half, local, ranks))
    return sample, gram.reshape(ranks, ranks)


def factor_block(a):
    size, wide = a.shape[0], 8
    shape = (wide, size)
    lane = lax.broadcasted_iota(jnp.int32, shape, 1)
    line = lax.broadcasted_iota(jnp.int32, shape, 0)

    def spread(x):
        return jnp.broadcast_to(x, shape)

    blocks = [a[i : i + wide] for i in range(0, size, wide)]
    upper, inverse = [], []
    for b in range(size // wide):
        at = b * wide
        inside = (lane >= at) & (lane < at + wide)
        x = blocks[b]
        y = jnp.where(inside, jnp.where(lane - at == line, 1.0, 0.0), x)
        marks = [spread(x[:, at + u : at + u + 1]) for u in range(wide)]
        over, root = jnp.zeros(shape, jnp.float32), jnp.zeros(shape, jnp.float32)
        for s in range(wide):
            pivot = spread(marks[s][s : s + 1])
            inv = 1.0 / pivot
            over = jnp.where(line == s, inv, over)
            root = jnp.where(line == s, pivot, root)
            if s + 1 < wide:
                low = jnp.where(line > s, marks[s] * inv, 0.0)
                for u in range(s + 1, wide):
                    marks[u] = marks[u] - low * spread(marks[u][s : s + 1])
                x = x - low * spread(x[s : s + 1])
                y = y - low * spread(y[s : s + 1])
        z = y * over
        for s in range(wide - 1, 0, -1):
            z = z - jnp.where(line < s, marks[s] * over, 0.0) * spread(z[s : s + 1])
        rows = [spread(z[t : t + 1]) for t in range(wide)]
        for i in range(b + 1, size // wide):
            old = blocks[i]
            parts = [spread(old[:, at + t : at + t + 1]) * rows[t] for t in range(wide)]
            while len(parts) > 1:
                parts = [p + q for p, q in zip(parts[::2], parts[1::2])]
            blocks[i] = jnp.where(inside, 0.0, old) - parts[0]
        root = lax.rsqrt(root)
        upper.append(jnp.where(lane >= at + line, x * root, 0.0))
        inverse.append(jnp.where(lane <= at + line, y * root, 0.0))
    return jnp.concatenate(upper, axis=0), jnp.concatenate(inverse, axis=0)


def finish_kernel(scale, gram, sample, basis, factor, up, low):
    ranks = gram.shape[0]
    half = ranks // 2
    mean = gram[...] * scale
    same = lax.broadcasted_iota(jnp.int32, (ranks, ranks), 0) == lax.broadcasted_iota(jnp.int32, (ranks, ranks), 1)
    trace = jnp.sum(jnp.sum(jnp.where(same, mean, 0.0), axis=1, keepdims=True), axis=0, keepdims=True)
    factor[...] = jnp.where(same, mean + (0.1 / ranks) * trace, mean)
    cross = factor[:half, half:]

    def one(index):
        start = pl.multiple_of(index * half, half)
        block = factor[pl.ds(start, half), pl.ds(start, half)]
        u, m = factor_block(block)
        up[index] = u
        low[index] = m

        @pl.when(index == 0)
        def _():
            lift = dot(m, cross, ((1,), (0,)))
            up[2] = lift
            factor[half:, half:] = factor[half:, half:] - dot(lift.T, lift, ((1,), (0,)))

    each(0, 2, one)
    lift = up[2]
    first = dot(sample[:, :half], low[0], ((1,), (1,)))
    second = dot(sample[:, half:] - dot(first, lift, ((1,), (0,))), low[1], ((1,), (1,)))
    basis[:, :half] = first
    basis[:, half:] = second
    factor[:half, :half] = up[0].T
    factor[:half, half:] = jnp.zeros((half, half), jnp.float32)
    factor[half:, :half] = lift.T
    factor[half:, half:] = up[1].T


def finish(gram, sample, everyone):
    ranks = gram.shape[0]
    half = ranks // 2
    return pl.pallas_call(
        functools.partial(finish_kernel, 1.0 / everyone),
        out_shape=(
            jax.ShapeDtypeStruct(sample.shape, jnp.float32),
            jax.ShapeDtypeStruct(gram.shape, jnp.float32),
        ),
        in_specs=[VMEM, VMEM],
        out_specs=(VMEM, VMEM),
        scratch_shapes=[pltpu.VMEM((3, half, half), jnp.float32), pltpu.VMEM((2, half, half), jnp.float32)],
        name="finish",
    )(gram, sample)


def body(rows, cols, points, sketch, rank, boundary, scales):
    sample, gram = reduce(tiles(points, sketch, rank, boundary, scales, rows, cols), rows, cols)
    return finish(gram, sample, rows * cols * points.shape[1])


def solution(mesh):
    placed = (P(None, ("row", "col")), P(("row", "col"), None), P(("row", "col")), P(), P())
    return jax.shard_map(
        functools.partial(body, mesh.shape["row"], mesh.shape["col"]),
        mesh=mesh,
        in_specs=placed,
        out_specs=(P(("row", "col"), None), P()),
        check_vma=False,
    )
```
